512 devices in a mesh: row: 32 (over z, core), inner: 16 (over x, y).
Axes of the slice: x: 4, y: 4, z: 16, core: 2. Of those that a mesh axis runs over, the one named last changes fastest.
Arguments:
- a_left: bfloat16 [32, 64, 1024, 128], P('row', 'inner'), may hold values from -0.5 to 0.5
- a_right: bfloat16 [32, 64, 1024, 128], P('row', 'inner'), may hold values from -0.1875 to 0.1875
- a_rank: int32 [32, 64], P('row', 'inner'), may hold values from 16 to 128, as said below
- b_left: bfloat16 [64, 4, 1024, 128], P('inner', None, 'row'), may hold values from -6 to 6
- b_right: bfloat16 [64, 4, 1024, 128], P('inner', None, 'row'), may hold values from -0.0625 to 0.0625
- b_rank: int32 [64, 4], P('inner'), may hold values from 16 to 128, as said below
- c_rank: int32 [32, 4], P('row'), may hold values from 16 to 128, as said below
- probes: bfloat16 [1024, 128], replicated, may hold values from -6 to 6
Outputs:
- q_basis: bfloat16 [32, 1024, 512], P('row', 'inner')
- w_factor: bfloat16 [32, 1024, 512], P('row', 'inner')
The draws below stay inside these ranges and needn't reach their ends.
Inputs may be any that keep to these rules, and one draw needn't show every extreme that they name: `a_rank`: A tile's factor columns at or beyond its rank are not used; some tile has rank 128 and some rank 128/8 in every draw. `b_rank`: likewise for the B tiles. `c_rank`: some C tile has target rank 128 and some 128/8 in every draw.
All inputs are finite; a program needn't handle non-finite values.
Results may differ from the reference program's by a relative error of at most 0.014.
Values may be sent and summed in bfloat16 or wider, within the bound.
A program may use at most 64 MiB of HBM per device.

```python
import jax
import jax.numpy as jnp
from jax import lax

NB = 1024
R = 128
P_SIZE = 128
COLS = 4
KT = 64
ROWT = 32


def ranks_with_ends(key, rows, columns, lowest, highest):
    values = jax.random.randint(key, (rows * columns,), lowest, highest + 1)
    where_top = jax.random.randint(jax.random.fold_in(key, 11), (), 0, rows * columns)
    where_low = (where_top + 1) % (rows * columns)
    values = values.at[where_top].set(highest).at[where_low].set(lowest)
    return values.reshape(rows, columns).astype(jnp.int32)


def draw_a_rank(key, part):
    return ranks_with_ends(jax.random.fold_in(key, 101), ROWT, KT, R // 8, R)


def draw_b_rank(key, part):
    return ranks_with_ends(jax.random.fold_in(key, 202), KT, COLS, R // 8, R)


def draw_c_rank(key, part):
    return ranks_with_ends(jax.random.fold_in(key, 303), ROWT, COLS, P_SIZE // 8, P_SIZE)


def steps_of(own_key, extent, split, least, high):
    level, own = 1.0, jax.random.fold_in(own_key, 6)
    for dim, shards_of in split:
        steps = jnp.exp(jax.random.uniform(jax.random.fold_in(own, dim), (shards_of,), jnp.float32, least / len(split), high / len(split)))
        level = level * jnp.repeat(steps, extent[dim] // shards_of).reshape([-1 if axis == dim else 1 for axis in range(len(extent))])
    return level


def centred(key, shape, width, limit, split=(), kind=jnp.bfloat16):
    drawn = width * jax.random.normal(key, shape, jnp.float32)
    if split:
        drawn = drawn * steps_of(key, shape, split, -0.22, 0.18)
    return jnp.clip(drawn, -limit, limit).astype(kind)


def setup_inputs(seed: int = 0) -> dict:
    key_list = jax.random.split(jax.random.key(seed), 9)
    a_left = centred(key_list[0], (ROWT, KT, NB, R), R ** -0.5, 0.5, ((0, 32), (1, 16)))
    a_right = centred(key_list[1], (ROWT, KT, NB, R), NB ** -0.5, 0.1875, ((0, 32), (1, 16)))
    a_rank = draw_a_rank(jax.random.fold_in(key_list[8], 71), 0)
    b_left = centred(key_list[3], (KT, COLS, NB, R), 1.0, 6.0, ((0, 16), (2, 32)))
    b_right = centred(key_list[4], (KT, COLS, NB, R), (R * KT) ** -0.5, 0.0625, ((0, 16), (2, 32)))
    b_rank = draw_b_rank(jax.random.fold_in(key_list[8], 71), 0)
    c_rank = draw_c_rank(jax.random.fold_in(key_list[8], 71), 0)
    probes = centred(key_list[7], (NB, P_SIZE), 1.0, 6.0)
    return dict(a_left=a_left, a_right=a_right, a_rank=a_rank, b_left=b_left, b_right=b_right, b_rank=b_rank, c_rank=c_rank, probes=probes)


def factor_basis(sketch_cols):
    gram_full = jnp.einsum('cnp,cnq->cpq', sketch_cols, sketch_cols, precision=lax.Precision.HIGHEST)
    diag_mean = lax.optimization_barrier(jnp.mean(jnp.diagonal(gram_full, axis1=1, axis2=2), axis=1))
    identity = jnp.eye(gram_full.shape[1], dtype=jnp.float32)
    gram_full = gram_full + 0.0001 * diag_mean[:, None, None] * identity[None]
    factor = jnp.linalg.cholesky(gram_full)

    def solve_one(factor_one, sketch_one):
        return jax.scipy.linalg.solve_triangular(factor_one, sketch_one.T, lower=True).T
    return jax.vmap(solve_one)(factor, sketch_cols)

def reference(a_left, a_right, a_rank, b_left, b_right, b_rank, c_rank, probes):
    rank_lane = jnp.arange(R)
    width_lane = jnp.arange(P_SIZE)
    keep_right = (rank_lane[None, None, :] < b_rank[:, :, None]).astype(jnp.float32)
    left_b = b_left.astype(jnp.float32)
    right_b = b_right.astype(jnp.float32)
    probed = jnp.einsum('kjnr,np->kjrp', right_b, probes.astype(jnp.float32))

    def one_row(packed):
        left_a, right_a, rank_a, rank_c = packed
        keep_left = (rank_lane[None, :] < rank_a[:, None]).astype(jnp.float32)
        core_block = jnp.einsum('knr,kjns->kjrs', right_a.astype(jnp.float32), left_b)
        core_block = core_block * keep_left[:, None, :, None] * keep_right[:, :, None, :]
        small_core = jnp.einsum('kjrs,kjsp->kjrp', core_block, probed, precision=lax.Precision.HIGHEST).astype(jnp.bfloat16)
        sketch = jnp.einsum('knr,kjrp->jnp', left_a.astype(jnp.float32), small_core.astype(jnp.float32))
        ortho = factor_basis(sketch)
        ortho = ortho * (width_lane[None, :] < rank_c[:, None]).astype(jnp.float32)[:, None, :]
        qround = ortho.astype(jnp.bfloat16)
        projected = jnp.einsum('jnp,knr->kjpr', qround.astype(jnp.float32), left_a.astype(jnp.float32))
        lifted = jnp.einsum('kjpr,kjrs->kjps', projected, core_block, precision=lax.Precision.HIGHEST).astype(jnp.bfloat16)
        coeff = jnp.einsum('kjns,kjps->jnp', right_b, lifted.astype(jnp.float32))
        basis_out = jnp.transpose(jnp.sqrt(jnp.float32(NB)) * ortho, (1, 0, 2)).reshape(NB, COLS * P_SIZE).astype(jnp.bfloat16)
        coeff_out = jnp.transpose(coeff, (1, 0, 2)).reshape(NB, COLS * P_SIZE).astype(jnp.bfloat16)
        return (basis_out, coeff_out)
    q_basis, w_factor = lax.map(one_row, (a_left, a_right, a_rank, c_rank))
    return (q_basis, w_factor)
```

```python
import functools

import jax
import jax.numpy as jnp
from jax import lax
from jax.experimental import pallas as pl
from jax.experimental.pallas import tpu as pltpu
from jax.sharding import PartitionSpec as P

MESH = pl.DeviceIdType.MESH
HIGH = lax.Precision.HIGHEST
F32 = jnp.float32
BF16 = jnp.bfloat16
SUB = 8
BLOCK = 32


def dot(a, b, dims=((1,), (0,)), precision=None):
    return lax.dot_general(
        a, b, (dims, ((), ())), precision=precision, preferred_element_type=F32
    )


def factor(work):
    size = work.shape[0]
    row_of = lax.broadcasted_iota(jnp.int32, (SUB, size), 0)
    for base in range(0, size, BLOCK):
        tiles = BLOCK // SUB
        left = [work[base + SUB * t : base + SUB * (t + 1), 0:size] for t in range(tiles)]
        right = [work[base + SUB * t : base + SUB * (t + 1), size : 2 * size] for t in range(tiles)]
        for b in range(tiles):
            start = base + SUB * b
            cols = [
                [
                    jnp.broadcast_to(left[t][:, start + j : start + j + 1], (SUB, size))
                    for j in range(SUB)
                ]
                for t in range(b, tiles)
            ]
            scale = jnp.ones((SUB, size), F32)
            for i in range(SUB):
                pivot = jnp.broadcast_to(cols[0][i][i : i + 1, :], (SUB, size))
                root = lax.rsqrt(pivot)
                inv = root * root
                scale = jnp.where(row_of == i, root, scale)
                row_l = jnp.broadcast_to(left[b][i : i + 1, :], (SUB, size))
                row_r = jnp.broadcast_to(right[b][i : i + 1, :], (SUB, size))
                row_c = [
                    jnp.broadcast_to(cols[0][j][i : i + 1, :], (SUB, size))
                    for j in range(i + 1, SUB)
                ]
                for t in range(b, tiles):
                    g = cols[t - b][i] * inv
                    if t == b:
                        g = jnp.where(row_of > i, g, 0.0)
                    left[t] = left[t] - g * row_l
                    right[t] = right[t] - g * row_r
                    for j in range(i + 1, SUB):
                        cols[t - b][j] = cols[t - b][j] - g * row_c[j - i - 1]
            left[b] = left[b] * scale
            right[b] = right[b] * scale
        for t in range(tiles):
            work[base + SUB * t : base + SUB * (t + 1), 0:size] = left[t]
            work[base + SUB * t : base + SUB * (t + 1), size : 2 * size] = right[t]
        rest = base + BLOCK
        if rest < size:
            rows = jnp.concatenate(
                [jnp.concatenate(left, axis=0), jnp.concatenate(right, axis=0)], axis=1
            )
            upper = jnp.concatenate(left, axis=0)
            turned = upper.T[rest:, :]
            work[rest:, :] = work[rest:, :] - dot(turned, rows, precision=HIGH)


def kernel(
    Z, X, Y,
    a_rank, b_rank, c_rank, al_hbm, ar_hbm, bl_hbm, br_hbm, pr_hbm,
    q_out, w_out,
    BL, BR, AL, AR, PR, ART, ALT, PT, CO, CT, SM, SB, RB, ROWS, GS, GR, WK, QB, PJ, LT, CB, WB,
    in_sem, zs, zr, ps, pr, rs, rr, gs, gr, qs, qr, ws, wr,
):
    KD, COLS, NB, R = BL.shape
    PW = PT.shape[0]
    shard = bl_hbm.shape[2]
    part = NB // X
    small_part = NB // (X * Y)
    pairs = COLS // 2
    r, q = lax.axis_index("row"), lax.axis_index("inner")
    z, c = r // 2, lax.rem(r, 2)
    x, y = q // Y, lax.rem(q, Y)
    up, down = lax.rem(z + 1, Z) * 2 + c, lax.rem(z + Z - 1, Z) * 2 + c
    mate = z * 2 + 1 - c
    peers = [(dx, dy) for dx in range(X) for dy in range(Y) if dx or dy]

    def peer(dx, dy):
        return lax.rem(x + dx, X), lax.rem(y + dy, Y)

    barrier = pltpu.get_barrier_semaphore()
    ring_peers = [up, down] if Z > 2 else [up]
    for other in ring_peers + [mate]:
        pl.semaphore_signal(barrier, 1, device_id={"row": other, "inner": q}, device_id_type=MESH)
    for dx, dy in peers:
        px, py = peer(dx, dy)
        pl.semaphore_signal(barrier, 1, device_id={"row": r, "inner": px * Y + py}, device_id_type=MESH)

    mine = pl.ds(pl.multiple_of(r * shard, shard), shard)
    loads = [
        pltpu.make_async_copy(bl_hbm, BL.at[:, :, mine, :], in_sem.at[0]),
        pltpu.make_async_copy(br_hbm, BR.at[:, :, mine, :], in_sem.at[1]),
        pltpu.make_async_copy(ar_hbm.at[0], AR, in_sem.at[2]),
        pltpu.make_async_copy(al_hbm.at[0], AL, in_sem.at[3]),
        pltpu.make_async_copy(pr_hbm, PR, in_sem.at[4]),
    ]
    for load in loads:
        load.start()
    pl.semaphore_wait(barrier, len(ring_peers) + 1 + len(peers))
    loads[0].wait()
    loads[1].wait()

    tensors = (BL, BR)
    long_steps, short_steps = Z // 2, (Z - 1) // 2
    steps = ((long_steps, short_steps), (short_steps, long_steps))

    def rows_of(origin, core):
        return pl.ds(pl.multiple_of((origin * 2 + core) * shard, shard), shard)

    def ring_copy(t, d, s, origin):
        ref = tensors[t].at[:, :, rows_of(origin, c), :]
        return pltpu.make_async_remote_copy(
            ref, ref, zs.at[t, d, s], zr.at[t, d, s],
            device_id={"row": down if d else up, "inner": q}, device_id_type=MESH,
        )

    def mate_copy(t, origin, core):
        ref = tensors[t].at[:, :, rows_of(origin, core), :]
        return pltpu.make_async_remote_copy(
            ref, ref, ps.at[t, origin], pr.at[t, origin],
            device_id={"row": mate, "inner": q}, device_id_type=MESH,
        )

    def sent_origin(d, s):
        return lax.rem(z + s, Z) if d else lax.rem(z + Z - s, Z)

    for t in range(2):
        for d in range(2):
            if steps[t][d]:
                ring_copy(t, d, 0, z).start()
    for t in range(2):
        mate_copy(t, z, c).start()

    loads[2].wait()
    loads[3].wait()
    loads[4].wait()

    def turn(k):
        at = pl.ds(pl.multiple_of(k * R, R), R)
        ART[at, :] = AR[k].T
        ALT[at, :] = AL[k].T

    def hop(s, forward):
        for t in range(2):
            for d in range(2):
                if isinstance(s, int) and s >= steps[t][d]:
                    continue
                origin = sent_origin(d, s + 1)
                ring_copy(t, d, s, origin).wait_recv()
                if forward or (isinstance(s, int) and s + 1 < steps[t][d]):
                    ring_copy(t, d, s + 1, origin).start()
                mate_copy(t, origin, c).start()

    def hop_loop(s, carry):
        hop(s, True)

        @pl.when(s < KD)
        def _():
            turn(s)

        return carry

    uniform = max(short_steps - 1, 0)
    lax.fori_loop(0, uniform, hop_loop, 0)
    for k in range(min(uniform, KD), KD):
        turn(k)
    PT[...] = PR[...].T
    for s in range(uniform, long_steps):
        hop(s, False)

    def mate_wait(t):
        def body(o, carry):
            mate_copy(t, o, 1 - c).wait_recv()
            return carry

        lax.fori_loop(0, Z, body, 0)

    mate_wait(0)
    mate_wait(1)

    row_lane = lax.broadcasted_iota(jnp.int32, (R, R), 0)
    col_lane = lax.broadcasted_iota(jnp.int32, (R, R), 1)

    def cores(k, carry):
        at = pl.ds(pl.multiple_of(k * R, R), R)
        lhs = ART[at, :]
        for g in range(pairs):
            j0 = 2 * g
            both = dot(lhs, jnp.concatenate([BL[k, j0], BL[k, j0 + 1]], axis=1))
            probed = dot(PT[...], jnp.concatenate([BR[k, j0], BR[k, j0 + 1]], axis=1))
            for h in range(2):
                j = j0 + h
                keep = jnp.logical_and(row_lane < a_rank[0, k], col_lane < b_rank[k, j])
                core = jnp.where(keep, both[:, h * R : (h + 1) * R], 0.0)
                CO[k, j] = core
                small = dot(core, probed[:, h * R : (h + 1) * R], ((1,), (1,)), HIGH)
                SM[at, j * PW : (j + 1) * PW] = small.astype(BF16)
        return carry

    lax.fori_loop(0, KD, cores, 0)

    def sketch_rows(px):
        at = pl.ds(pl.multiple_of(px * part, part), part)
        lhs = jnp.concatenate([AL[k, at, :] for k in range(KD)], axis=1)
        rows = dot(lhs, SM[...])
        for j in range(COLS):
            SB[px * Y + j] = rows[:, j * PW : (j + 1) * PW].astype(BF16)

    def block_copy(src, dst, send, recv, e, target):
        return pltpu.make_async_remote_copy(
            src.at[target], dst.at[e], send.at[e], recv.at[e],
            device_id={"row": r, "inner": target}, device_id_type=MESH,
        )

    def send_column(dx, src, dst, send, recv, first):
        def body(dy, carry):
            px, py = lax.rem(x + dx, X), lax.rem(y + dy, Y)
            block_copy(src, dst, send, recv, dx * Y + dy, px * Y + py).start()
            return carry

        lax.fori_loop(first, Y, body, 0)

    def sketch_loop(dx, carry):
        sketch_rows(lax.rem(x + dx, X))
        send_column(dx, SB, RB, rs, rr, 0)
        return carry

    lax.fori_loop(1, X, sketch_loop, 0)
    sketch_rows(x)
    send_column(0, SB, RB, rs, rr, 1)

    def turn_cores(k, carry):
        for j in range(COLS):
            CT[k, j] = CO[k, j].T
        return carry

    lax.fori_loop(0, KD, turn_cores, 0)

    def gather_sum(src, dst, send, recv):
        total = src[q].astype(F32)
        for e in range(1, X * Y):
            block_copy(src, dst, send, recv, e, q).wait_recv()
            total = total + dst[e].astype(F32)
        return total

    ROWS[...] = gather_sum(SB, RB, rs, rr)

    own_rows = ROWS[...]
    GS[...] = dot(own_rows.T, own_rows, precision=HIGH)

    def gram_copy(dx):
        px = lax.rem(x + dx, X)
        return pltpu.make_async_remote_copy(
            GS, GR.at[dx], gs.at[dx], gr.at[dx],
            device_id={"row": r, "inner": px * Y + y}, device_id_type=MESH,
        )

    for dx in range(1, X):
        gram_copy(dx).start()
    gram = GS[...]
    for dx in range(1, X):
        gram_copy(dx).wait_recv()
        gram = gram + GR[dx]
    eye = row_lane == col_lane
    mean = jnp.sum(jnp.where(eye, gram, 0.0), keepdims=True) / PW
    gram = gram + jnp.where(eye, 0.0001 * mean, 0.0)
    WK[:, 0:PW] = gram
    WK[:, PW : 2 * PW] = jnp.where(eye, 1.0, 0.0)
    factor(WK)
    basis = dot(ROWS[...], WK[:, PW : 2 * PW], ((1,), (1,)), HIGH)
    lane = lax.broadcasted_iota(jnp.int32, basis.shape, 1)
    basis = jnp.where(lane < c_rank[0, y], basis, 0.0)
    own_at = pl.ds(pl.multiple_of(x * part, part), part)
    QB[y, own_at, :] = basis.astype(BF16)

    def basis_copy(e, sx, sy, px, py):
        ref = QB.at[sy, pl.ds(pl.multiple_of(sx * part, part), part), :]
        return pltpu.make_async_remote_copy(
            ref, ref, qs.at[e], qr.at[e],
            device_id={"row": r, "inner": px * Y + py}, device_id_type=MESH,
        )

    for dx, dy in peers:
        px, py = peer(dx, dy)
        basis_copy(dx * Y + dy, x, y, px, py).start()
    for dx, dy in peers:
        sx, sy = lax.rem(x + X - dx, X), lax.rem(y + Y - dy, Y)
        basis_copy(dx * Y + dy, sx, sy, x, y).wait_recv()

    out_at = pl.ds(pl.multiple_of(q * small_part, small_part), small_part)
    for j in range(COLS):
        q_out[0, :, j * PW : (j + 1) * PW] = (
            jnp.sqrt(jnp.float32(NB)) * QB[j, out_at, :].astype(F32)
        ).astype(BF16)

    for g in range(pairs):
        PJ[:, 2 * g * PW : (2 * g + 2) * PW] = dot(
            ALT[...], jnp.concatenate([QB[2 * g], QB[2 * g + 1]], axis=1)
        )

    def lift(k, carry):
        at = pl.ds(pl.multiple_of(k * R, R), R)
        for j in range(COLS):
            lifted = dot(CT[k, j], PJ[at, j * PW : (j + 1) * PW], precision=HIGH)
            LT[at, j * PW : (j + 1) * PW] = lifted.astype(BF16)
        return carry

    lax.fori_loop(0, KD, lift, 0)

    def coeff_rows(px):
        at = pl.ds(pl.multiple_of(px * part, part), part)
        for j in range(COLS):
            lhs = jnp.concatenate([BR[k, j, at, :] for k in range(KD)], axis=1)
            rows = dot(lhs, LT[:, j * PW : (j + 1) * PW]).astype(BF16)
            for h in range(Y):
                CB[px * Y + h, :, j * PW : (j + 1) * PW] = rows[h * small_part : (h + 1) * small_part, :]

    def coeff_loop(dx, carry):
        coeff_rows(lax.rem(x + dx, X))
        send_column(dx, CB, WB, ws, wr, 0)
        return carry

    lax.fori_loop(1, X, coeff_loop, 0)
    coeff_rows(x)
    send_column(0, CB, WB, ws, wr, 1)
    w_out[0] = gather_sum(CB, WB, ws, wr).astype(BF16)

    for t in range(2):
        for d in range(2):
            for s in range(steps[t][d]):
                ring_copy(t, d, s, z).wait_send()

        def sent(o, carry):
            mate_copy(t, o, c).wait_send()
            return carry

        lax.fori_loop(0, Z, sent, 0)
    for e in range(1, X * Y):
        block_copy(SB, RB, rs, rr, e, q).wait_send()
        basis_copy(e, x, y, x, y).wait_send()
        block_copy(CB, WB, ws, wr, e, q).wait_send()
    for dx in range(1, X):
        gram_copy(dx).wait_send()


def per_device(Z, X, Y, a_left, a_right, a_rank, b_left, b_right, b_rank, c_rank, probes):
    _, KD, NB, R = a_left.shape
    COLS = b_left.shape[1]
    PW = probes.shape[1]
    part, small_part = NB // X, NB // (X * Y)
    n = X * Y
    long_steps = max(Z // 2, 1)
    any_space = pl.BlockSpec(memory_space=pl.ANY)
    smem = pl.BlockSpec(memory_space=pltpu.SMEM)
    vmem = pl.BlockSpec(memory_space=pltpu.VMEM)
    dma = pltpu.SemaphoreType.DMA
    V = pltpu.VMEM
    out = jax.ShapeDtypeStruct((1, small_part, COLS * PW), BF16)
    return pl.pallas_call(
        functools.partial(kernel, Z, X, Y),
        out_shape=(out, out),
        in_specs=[smem] * 3 + [any_space] * 5,
        out_specs=(vmem, vmem),
        scratch_shapes=[
            V((KD, COLS, NB, R), BF16),
            V((KD, COLS, NB, R), BF16),
            V((KD, NB, R), BF16),
            V((KD, NB, R), BF16),
            V((NB, PW), BF16),
            V((KD * R, NB), BF16),
            V((KD * R, NB), BF16),
            V((PW, NB), BF16),
            V((KD, COLS, R, R), F32),
            V((KD, COLS, R, R), F32),
            V((KD * R, COLS * PW), BF16),
            V((n, part, PW), BF16),
            V((n, part, PW), BF16),
            V((part, PW), F32),
            V((PW, PW), F32),
            V((X, PW, PW), F32),
            V((PW, 2 * PW), F32),
            V((COLS, NB, PW), BF16),
            V((KD * R, COLS * PW), F32),
            V((KD * R, COLS * PW), BF16),
            V((n, small_part, COLS * PW), BF16),
            V((n, small_part, COLS * PW), BF16),
            dma((5,)),
            dma((2, 2, long_steps)), dma((2, 2, long_steps)),
            dma((2, Z)), dma((2, Z)),
            dma((n,)), dma((n,)),
            dma((X,)), dma((X,)),
            dma((n,)), dma((n,)),
            dma((n,)), dma((n,)),
        ],
        compiler_params=pltpu.CompilerParams(collective_id=0, has_side_effects=True),
    )(a_rank, b_rank, c_rank, a_left, a_right, b_left, b_right, probes)


def solution(mesh):
    Z = mesh.shape["row"] // 2
    Y = 4
    X = mesh.shape["inner"] // Y
    return jax.shard_map(
        functools.partial(per_device, Z, X, Y),
        mesh=mesh,
        in_specs=(
            P("row", "inner", None, None),
            P("row", "inner", None, None),
            P("row", "inner"),
            P("inner", None, "row", None),
            P("inner", None, "row", None),
            P("inner", None),
            P("row", None),
            P(),
        ),
        out_specs=(P("row", "inner", None), P("row", "inner", None)),
        check_vma=False,
    )
```

```python
import functools

import jax
import jax.numpy as jnp
from jax import lax
from jax.experimental import pallas as pl
from jax.experimental.pallas import tpu as pltpu
from jax.sharding import PartitionSpec as P

MESH = pl.DeviceIdType.MESH
HIGH = lax.Precision.HIGHEST
F32 = jnp.float32
BF16 = jnp.bfloat16
SUB = 8
CHUNKS = 2
BLOCK = 32


def dot(a, b, dims=((1,), (0,)), precision=None):
    return lax.dot_general(
        a, b, (dims, ((), ())), precision=precision, preferred_element_type=F32
    )


def factor(work):
    size = work.shape[0]
    row_of = lax.broadcasted_iota(jnp.int32, (SUB, size), 0)
    for base in range(0, size, BLOCK):
        tiles = BLOCK // SUB
        left = [work[base + SUB * t : base + SUB * (t + 1), 0:size] for t in range(tiles)]
        right = [work[base + SUB * t : base + SUB * (t + 1), size : 2 * size] for t in range(tiles)]
        for b in range(tiles):
            start = base + SUB * b
            cols = [
                [
                    jnp.broadcast_to(left[t][:, start + j : start + j + 1], (SUB, size))
                    for j in range(SUB)
                ]
                for t in range(b, tiles)
            ]
            scale = jnp.ones((SUB, size), F32)
            for i in range(SUB):
                pivot = jnp.broadcast_to(cols[0][i][i : i + 1, :], (SUB, size))
                root = lax.rsqrt(pivot)
                inv = root * root
                scale = jnp.where(row_of == i, root, scale)
                row_l = jnp.broadcast_to(left[b][i : i + 1, :], (SUB, size))
                row_r = jnp.broadcast_to(right[b][i : i + 1, :], (SUB, size))
                row_c = [
                    jnp.broadcast_to(cols[0][j][i : i + 1, :], (SUB, size))
                    for j in range(i + 1, SUB)
                ]
                for t in range(b, tiles):
                    g = cols[t - b][i] * inv
                    if t == b:
                        g = jnp.where(row_of > i, g, 0.0)
                    left[t] = left[t] - g * row_l
                    right[t] = right[t] - g * row_r
                    for j in range(i + 1, SUB):
                        cols[t - b][j] = cols[t - b][j] - g * row_c[j - i - 1]
            left[b] = left[b] * scale
            right[b] = right[b] * scale
        for t in range(tiles):
            work[base + SUB * t : base + SUB * (t + 1), 0:size] = left[t]
            work[base + SUB * t : base + SUB * (t + 1), size : 2 * size] = right[t]
        rest = base + BLOCK
        if rest < size:
            rows = jnp.concatenate(
                [jnp.concatenate(left, axis=0), jnp.concatenate(right, axis=0)], axis=1
            )
            upper = jnp.concatenate(left, axis=0)
            turned = upper.T[rest:, :]
            work[rest:, :] = work[rest:, :] - dot(turned, rows, precision=HIGH)


def kernel(
    Z, X, Y,
    a_rank, b_rank, c_rank, al_hbm, ar_hbm, bl_hbm, br_hbm, pr_hbm,
    q_out, w_out,
    BL, BR, AL, AR, PR, ALT, PB, CO, CT, SM, SF, SG, ST, SU, ROWS, GS, GR, WK, NI, QB, PJ, LT, CF, CG, CT2, CU,
    in_sem, zs, zr, ps, pr, rs, rr, gs, gr, ns, nr, qs, qr,
):
    KD, COLS, NB, R = BL.shape
    PW = PR.shape[1]
    shard = bl_hbm.shape[2]
    part = NB // X
    halfpart = part // 2
    small_part = NB // (X * Y)
    pairs = COLS // 2
    r, q = lax.axis_index("row"), lax.axis_index("inner")
    z, c = r // 2, lax.rem(r, 2)
    x, y = q // Y, lax.rem(q, Y)
    up, down = lax.rem(z + 1, Z) * 2 + c, lax.rem(z + Z - 1, Z) * 2 + c
    mate = z * 2 + 1 - c
    peers = [(dx, dy) for dx in range(X) for dy in range(Y) if dx or dy]

    def peer(dx, dy):
        return lax.rem(x + dx, X), lax.rem(y + dy, Y)

    barrier = pltpu.get_barrier_semaphore()
    ring_peers = [up, down] if Z > 2 else [up]
    for other in ring_peers + [mate]:
        pl.semaphore_signal(barrier, 1, device_id={"row": other, "inner": q}, device_id_type=MESH)
    for dx, dy in peers:
        px, py = peer(dx, dy)
        pl.semaphore_signal(barrier, 1, device_id={"row": r, "inner": px * Y + py}, device_id_type=MESH)

    mine = pl.ds(pl.multiple_of(r * shard, shard), shard)
    loads = [
        pltpu.make_async_copy(bl_hbm, BL.at[:, :, mine, :], in_sem.at[0]),
        pltpu.make_async_copy(br_hbm, BR.at[:, :, mine, :], in_sem.at[1]),
        pltpu.make_async_copy(ar_hbm.at[0], AR, in_sem.at[2]),
        pltpu.make_async_copy(al_hbm.at[0], AL, in_sem.at[3]),
        pltpu.make_async_copy(pr_hbm, PR, in_sem.at[4]),
    ]
    for load in loads:
        load.start()
    pl.semaphore_wait(barrier, len(ring_peers) + 1 + len(peers))

    tensors, given = (BL, BR), (bl_hbm, br_hbm)
    long_steps, short_steps = Z // 2, (Z - 1) // 2
    steps = ((long_steps, short_steps), (short_steps, long_steps))

    def rows_of(origin, core):
        return pl.ds(pl.multiple_of((origin * 2 + core) * shard, shard), shard)

    half = KD // CHUNKS

    def ring_copy(t, h, d, s, origin, own=False):
        ref = tensors[t].at[h * half : (h + 1) * half, :, rows_of(origin, c), :]
        src = given[t].at[h * half : (h + 1) * half] if own else ref
        return pltpu.make_async_remote_copy(
            src, ref, zs.at[t, h, d, s], zr.at[t, h, d, s],
            device_id={"row": down if d else up, "inner": q}, device_id_type=MESH,
        )

    def mate_copy(t, h, origin, core, own=False):
        ref = tensors[t].at[h * half : (h + 1) * half, :, rows_of(origin, core), :]
        src = given[t].at[h * half : (h + 1) * half] if own else ref
        return pltpu.make_async_remote_copy(
            src, ref, ps.at[t, h, origin], pr.at[t, h, origin],
            device_id={"row": mate, "inner": q}, device_id_type=MESH,
        )

    def sent_origin(d, s):
        return lax.rem(z + s, Z) if d else lax.rem(z + Z - s, Z)

    chunks = [(t, h) for t in range(2) for h in range(CHUNKS)]
    for t, h in chunks:
        for d in range(2):
            if steps[t][d]:
                ring_copy(t, h, d, 0, z, True).start()
    for t, h in chunks:
        mate_copy(t, h, z, c, True).start()

    loads[0].wait()
    loads[1].wait()
    loads[2].wait()
    loads[3].wait()
    loads[4].wait()
    CO[...] = jnp.zeros(CO.shape, F32)
    PB[...] = jnp.zeros(PB.shape, F32)

    def turn(k):
        at = pl.ds(pl.multiple_of(k * R, R), R)
        ALT[at, :] = AL[k].T

    def mate_wait(origins):
        for o in origins:
            for t, h in chunks:
                mate_copy(t, h, o, 1 - c).wait_recv()

    def absorb(origins):
        ats = [pl.ds(pl.multiple_of(o * 2 * shard, 2 * shard), 2 * shard) for o in origins]

        def stack(parts):
            return jnp.concatenate(parts, axis=0) if len(parts) > 1 else parts[0]

        probe = stack([PR[at, :] for at in ats]).T

        def body(k, carry):
            lhs = stack([AR[k, at, :] for at in ats]).T
            for g in range(pairs):
                for ref, left, total in ((BL, lhs, CO), (BR, probe, PB)):
                    rhs = jnp.concatenate(
                        [stack([ref[k, 2 * g + h, at, :] for at in ats]) for h in range(2)], axis=1
                    )
                    total[k, g] += dot(left, rhs)
            return carry

        lax.fori_loop(0, KD, body, 0)

    def hop(s, forward):
        for t, h in chunks:
            for d in range(2):
                if isinstance(s, int) and s >= steps[t][d]:
                    continue
                origin = sent_origin(d, s + 1)
                ring_copy(t, h, d, s, origin).wait_recv()
                if forward or (isinstance(s, int) and s + 1 < steps[t][d]):
                    ring_copy(t, h, d, s + 1, origin).start()
                mate_copy(t, h, origin, c).start()

    def both(s):
        return sent_origin(0, s), sent_origin(1, s)

    uniform = max(short_steps - 1, 0)
    if uniform:
        hop(0, True)
        mate_wait([z])
        absorb([z])

        def hop_loop(s, carry):
            hop(s, True)

            @pl.when(s < KD + 1)
            def _():
                turn(s - 1)

            mate_wait(both(s))
            absorb(both(s))
            return carry

        lax.fori_loop(1, uniform, hop_loop, 0)
        for k in range(min(uniform - 1, KD), KD):
            turn(k)
        done = uniform
    else:
        for k in range(KD):
            turn(k)
        mate_wait([z])
        absorb([z])
        done = 1
    for s in range(uniform, long_steps):
        hop(s, False)
        if 1 <= s:
            mate_wait(both(s))
            absorb(both(s))
    if Z > 1:
        last = [sent_origin(0, long_steps)]
        if short_steps == long_steps:
            last.append(sent_origin(1, long_steps))
        mate_wait(last)
        absorb(last)

    row_lane = lax.broadcasted_iota(jnp.int32, (R, R), 0)
    col_lane = lax.broadcasted_iota(jnp.int32, (R, R), 1)

    def cores(k, carry):
        at = pl.ds(pl.multiple_of(k * R, R), R)
        for j in range(COLS):
            g, at_j = j // 2, slice((j % 2) * R, (j % 2 + 1) * R)
            keep = jnp.logical_and(row_lane < a_rank[0, k], col_lane < b_rank[k, j])
            core = jnp.where(keep, CO[k, g, :, at_j], 0.0)
            CO[k, g, :, at_j] = core
            small = dot(core, PB[k, g, :, at_j], ((1,), (1,)), HIGH)
            SM[at, j * PW : (j + 1) * PW] = small.astype(BF16)
        return carry

    lax.fori_loop(0, KD, cores, 0)

    size, me = (X, Y), (x, y)

    def line(p, d):
        px, py = (lax.rem(x + d, X), y) if p == 0 else (x, lax.rem(y + d, Y))
        return {"row": r, "inner": px * Y + py}

    def first_copy(i, F, G, p, d):
        return pltpu.make_async_remote_copy(
            F.at[p, lax.rem(me[p] + d, size[p])], G.at[p, d], rs.at[i, 0, p, d], rr.at[i, 0, p, d],
            device_id=line(p, d), device_id_type=MESH,
        )

    def second_copy(i, T, U, p, d):
        return pltpu.make_async_remote_copy(
            T.at[p, lax.rem(me[1 - p] + d, size[1 - p])], U.at[p, d], rs.at[i, 1, p, d], rr.at[i, 1, p, d],
            device_id=line(1 - p, d), device_id_type=MESH,
        )

    def spread(i, compute, F, G):
        def body(d, carry):
            compute(lax.rem(x + d, X))
            first_copy(i, F, G, 0, d).start()
            return carry

        lax.fori_loop(1, X, body, 0)
        compute(x)
        for d in range(1, Y):
            first_copy(i, F, G, 1, d).start()

    def middle(i, F, G, T, U):
        for p in range(2):
            for d in range(1, size[p]):
                first_copy(i, F, G, p, d).wait_recv()

            def body(d, carry):
                o = lax.rem(me[1 - p] + d, size[1 - p])
                total = F[p, me[p], o].astype(F32)
                for e in range(1, size[p]):
                    total = total + G[p, e, o].astype(F32)
                T[p, o] = total.astype(BF16)
                return carry

            lax.fori_loop(1, size[1 - p] + 1, body, 0)
            for d in range(1, size[1 - p]):
                second_copy(i, T, U, p, d).start()

    def final(i, T, U, p):
        total = T[p, me[1 - p]].astype(F32)
        for d in range(1, size[1 - p]):
            second_copy(i, T, U, p, d).wait_recv()
            total = total + U[p, d].astype(F32)
        return total

    def sketch_rows(px):
        at = pl.ds(pl.multiple_of(px * part, part), part)
        lhs = jnp.concatenate([AL[k, at, :] for k in range(KD)], axis=1)
        rows = dot(lhs, SM[...]).astype(BF16)
        for j in range(COLS):
            SF[0, px, j] = rows[:halfpart, j * PW : (j + 1) * PW]
            SF[1, j, px] = rows[halfpart:, j * PW : (j + 1) * PW]

    spread(0, sketch_rows, SF, SG)

    def turn_cores(k, carry):
        for j in range(COLS):
            CT[k, j] = CO[k, j // 2, :, (j % 2) * R : (j % 2 + 1) * R].T
        return carry

    lax.fori_loop(0, KD, turn_cores, 0)

    middle(0, SF, SG, ST, SU)
    for p in range(2):
        ROWS[p * halfpart : (p + 1) * halfpart, :] = final(0, ST, SU, p)

    own_rows = ROWS[...]
    GS[...] = dot(own_rows.T, own_rows, precision=HIGH)

    def gram_copy(dx):
        px = lax.rem(x + dx, X)
        return pltpu.make_async_remote_copy(
            GS, GR.at[dx], gs.at[dx], gr.at[dx],
            device_id={"row": r, "inner": px * Y + y}, device_id_type=MESH,
        )

    for dx in range(1, X):
        gram_copy(dx).start()

    for p in range(2):
        QB[y, x, p] = own_rows[p * halfpart : (p + 1) * halfpart, :].astype(BF16)

    def share_copy(step, p, d, sx, sy):
        if step == 0:
            ref = QB.at[sy, sx, p]
        else:
            ref = QB.at[sy, :, 0] if p == 0 else QB.at[:, sx, 1]
        return pltpu.make_async_remote_copy(
            ref, ref, qs.at[step, p, d], qr.at[step, p, d],
            device_id=line(p if step == 0 else 1 - p, d), device_id_type=MESH,
        )

    def share_wait(step, p):
        along = p if step == 0 else 1 - p
        for d in range(1, size[along]):
            sx = lax.rem(x + X - d, X) if along == 0 else x
            sy = lax.rem(y + Y - d, Y) if along == 1 else y
            share_copy(step, p, d, sx, sy).wait_recv()

    def share_start(step, p):
        for d in range(1, size[p if step == 0 else 1 - p]):
            share_copy(step, p, d, x, y).start()

    share_start(0, 0)
    share_start(0, 1)
    for p in range(2):
        share_wait(0, p)
        share_start(1, p)

    gram = GS[...]
    for dx in range(1, X):
        gram_copy(dx).wait_recv()
        gram = gram + GR[dx]
    eye = row_lane == col_lane
    mean = jnp.sum(jnp.where(eye, gram, 0.0), keepdims=True) / PW
    gram = gram + jnp.where(eye, 0.0001 * mean, 0.0)
    WK[:, 0:PW] = gram
    WK[:, PW : 2 * PW] = jnp.where(eye, 1.0, 0.0)
    factor(WK)
    NI[y] = WK[:, PW : 2 * PW]

    def inverse_copy(dy, sy, py):
        return pltpu.make_async_remote_copy(
            NI.at[sy], NI.at[sy], ns.at[dy], nr.at[dy],
            device_id={"row": r, "inner": x * Y + py}, device_id_type=MESH,
        )

    for dy in range(1, Y):
        inverse_copy(dy, y, lax.rem(y + dy, Y)).start()
    for p in range(2):
        share_wait(1, p)

    for g in range(pairs):
        PJ[:, 2 * g * PW : (2 * g + 2) * PW] = dot(
            ALT[...], jnp.concatenate([QB[2 * g + h].reshape(NB, PW) for h in range(2)], axis=1)
        )
    for dy in range(1, Y):
        inverse_copy(dy, lax.rem(y + Y - dy, Y), y).wait_recv()

    def orthonormal(rows, j):
        turned = dot(rows, NI[j], ((1,), (1,)), HIGH)
        lane = lax.broadcasted_iota(jnp.int32, turned.shape, 1)
        return jnp.where(lane < c_rank[0, j], turned, 0.0)

    for j in range(COLS):
        at_j = slice(j * PW, (j + 1) * PW)
        PJ[:, at_j] = orthonormal(PJ[:, at_j], j)

    def lift(k, carry):
        at = pl.ds(pl.multiple_of(k * R, R), R)
        for j in range(COLS):
            lifted = dot(CT[k, j], PJ[at, j * PW : (j + 1) * PW], precision=HIGH)
            LT[at, j * PW : (j + 1) * PW] = lifted.astype(BF16)
        return carry

    lax.fori_loop(0, KD, lift, 0)

    def coeff_rows(px):
        at = pl.ds(pl.multiple_of(px * part, part), part)
        cut = small_part // 2
        for j in range(COLS):
            at_j = slice(j * PW, (j + 1) * PW)
            lhs = jnp.concatenate([BR[k, j, at, :] for k in range(KD)], axis=1)
            rows = dot(lhs, LT[:, at_j]).astype(BF16)
            for h in range(Y):
                CF[0, px, h, :, at_j] = rows[h * small_part : h * small_part + cut, :]
                CF[1, h, px, :, at_j] = rows[h * small_part + cut : (h + 1) * small_part, :]

    spread(1, coeff_rows, CF, CG)
    for j in range(COLS):
        at_q = pl.ds(pl.multiple_of(lax.rem(y, Y // 2) * small_part, small_part), small_part)
        own = orthonormal(QB[j, x, y // (Y // 2), at_q, :].astype(F32), j)
        q_out[:, j * PW : (j + 1) * PW] = jnp.sqrt(jnp.float32(NB)) * own
    middle(1, CF, CG, CT2, CU)
    for p in range(2):
        cut = small_part // 2
        w_out[p * cut : (p + 1) * cut, :] = final(1, CT2, CU, p)

    for t, h in chunks:
        for d in range(2):
            for s in range(steps[t][d]):
                ring_copy(t, h, d, s, z).wait_send()

        def sent(o, carry):
            mate_copy(t, h, o, c).wait_send()
            return carry

        lax.fori_loop(0, Z, sent, 0)
    for p in range(2):
        for i, (F, G, T, U) in enumerate(((SF, SG, ST, SU), (CF, CG, CT2, CU))):
            for d in range(1, size[p]):
                first_copy(i, F, G, p, d).wait_send()
            for d in range(1, size[1 - p]):
                second_copy(i, T, U, p, d).wait_send()
        for step in range(2):
            for d in range(1, size[p if step == 0 else 1 - p]):
                share_copy(step, p, d, x, y).wait_send()
    for dx in range(1, X):
        gram_copy(dx).wait_send()
    for dy in range(1, Y):
        inverse_copy(dy, y, y).wait_send()


def per_device(Z, X, Y, a_left, a_right, a_rank, b_left, b_right, b_rank, c_rank, probes):
    _, KD, NB, R = a_left.shape
    COLS = b_left.shape[1]
    PW = probes.shape[1]
    part, small_part = NB // X, NB // (X * Y)
    m, half = max(X, Y), part // 2
    long_steps = max(Z // 2, 1)
    any_space = pl.BlockSpec(memory_space=pl.ANY)
    smem = pl.BlockSpec(memory_space=pltpu.SMEM)
    vmem = pl.BlockSpec(memory_space=pltpu.VMEM)
    dma = pltpu.SemaphoreType.DMA
    V = pltpu.VMEM
    out = jax.ShapeDtypeStruct((small_part, COLS * PW), F32)
    q_basis, w_factor = pl.pallas_call(
        functools.partial(kernel, Z, X, Y),
        out_shape=(out, out),
        in_specs=[smem] * 3 + [any_space] * 5,
        out_specs=(vmem, vmem),
        scratch_shapes=[
            V((KD, COLS, NB, R), BF16),
            V((KD, COLS, NB, R), BF16),
            V((KD, NB, R), BF16),
            V((KD, NB, R), BF16),
            V((NB, PW), BF16),
            V((KD * R, NB), BF16),
            V((KD, COLS // 2, PW, 2 * R), F32),
            V((KD, COLS // 2, R, 2 * R), F32),
            V((KD, COLS, R, R), F32),
            V((KD * R, COLS * PW), BF16),
            V((2, m, m, half, PW), BF16),
            V((2, m, m, half, PW), BF16),
            V((2, m, half, PW), BF16),
            V((2, m, half, PW), BF16),
            V((part, PW), F32),
            V((PW, PW), F32),
            V((X, PW, PW), F32),
            V((PW, 2 * PW), F32),
            V((COLS, PW, PW), F32),
            V((COLS, X, 2, half, PW), BF16),
            V((KD * R, COLS * PW), F32),
            V((KD * R, COLS * PW), BF16),
            V((2, m, m, small_part // 2, COLS * PW), BF16),
            V((2, m, m, small_part // 2, COLS * PW), BF16),
            V((2, m, small_part // 2, COLS * PW), BF16),
            V((2, m, small_part // 2, COLS * PW), BF16),
            dma((5,)),
            dma((2, CHUNKS, 2, long_steps)), dma((2, CHUNKS, 2, long_steps)),
            dma((2, CHUNKS, Z)), dma((2, CHUNKS, Z)),
            dma((2, 2, 2, m)), dma((2, 2, 2, m)),
            dma((X,)), dma((X,)),
            dma((Y,)), dma((Y,)),
            dma((2, 2, m)), dma((2, 2, m)),
        ],
        compiler_params=pltpu.CompilerParams(collective_id=0, has_side_effects=True),
    )(a_rank, b_rank, c_rank, a_left, a_right, b_left, b_right, probes)
    return q_basis.astype(BF16)[None], w_factor.astype(BF16)[None]


def solution(mesh):
    Z = mesh.shape["row"] // 2
    Y = 4
    X = mesh.shape["inner"] // Y
    return jax.shard_map(
        functools.partial(per_device, Z, X, Y),
        mesh=mesh,
        in_specs=(
            P("row", "inner", None, None),
            P("row", "inner", None, None),
            P("row", "inner"),
            P("inner", None, "row", None),
            P("inner", None, "row", None),
            P("inner", None),
            P("row", None),
            P(),
        ),
        out_specs=(P("row", "inner", None), P("row", "inner", None)),
        check_vma=False,
    )
```

```python
import functools

import jax
import jax.numpy as jnp
from jax import lax
from jax.experimental import pallas as pl
from jax.experimental.pallas import tpu as pltpu
from jax.sharding import PartitionSpec as P

MESH = pl.DeviceIdType.MESH
HIGH = lax.Precision.HIGHEST
F32 = jnp.float32
BF16 = jnp.bfloat16
SUB = 8
CHUNKS = 2
BLOCK = 32


def dot(a, b, dims=((1,), (0,)), precision=None):
    return lax.dot_general(
        a, b, (dims, ((), ())), precision=precision, preferred_element_type=F32
    )


def split(v):
    high = v.astype(BF16)
    return high, (v - high.astype(F32)).astype(BF16)


def dot3(a, b, dims=((1,), (0,))):
    (ah, al), (bh, bl) = split(a), split(b)
    return dot(
        jnp.concatenate([ah, ah, al], axis=dims[0][0]),
        jnp.concatenate([bh, bl, bh], axis=dims[1][0]),
        dims,
    )


def factor(work):
    size = work.shape[0]
    row_of = lax.broadcasted_iota(jnp.int32, (SUB, size), 0)
    for base in range(0, size, BLOCK):
        tiles = BLOCK // SUB
        left = [work[base + SUB * t : base + SUB * (t + 1), 0:size] for t in range(tiles)]
        right = [work[base + SUB * t : base + SUB * (t + 1), size : 2 * size] for t in range(tiles)]
        for b in range(tiles):
            start = base + SUB * b
            cols = [
                [
                    jnp.broadcast_to(left[t][:, start + j : start + j + 1], (SUB, size))
                    for j in range(SUB)
                ]
                for t in range(b, tiles)
            ]
            scale = jnp.ones((SUB, size), F32)
            for i in range(SUB):
                pivot = jnp.broadcast_to(cols[0][i][i : i + 1, :], (SUB, size))
                root = lax.rsqrt(pivot)
                inv = root * root
                scale = jnp.where(row_of == i, root, scale)
                row_l = jnp.broadcast_to(left[b][i : i + 1, :], (SUB, size))
                row_r = jnp.broadcast_to(right[b][i : i + 1, :], (SUB, size))
                row_c = [
                    jnp.broadcast_to(cols[0][j][i : i + 1, :], (SUB, size))
                    for j in range(i + 1, SUB)
                ]
                for t in range(b, tiles):
                    g = cols[t - b][i] * inv
                    if t == b:
                        g = jnp.where(row_of > i, g, 0.0)
                    left[t] = left[t] - g * row_l
                    right[t] = right[t] - g * row_r
                    for j in range(i + 1, SUB):
                        cols[t - b][j] = cols[t - b][j] - g * row_c[j - i - 1]
            left[b] = left[b] * scale
            right[b] = right[b] * scale
        for t in range(tiles):
            work[base + SUB * t : base + SUB * (t + 1), 0:size] = left[t]
            work[base + SUB * t : base + SUB * (t + 1), size : 2 * size] = right[t]
        rest = base + BLOCK
        if rest < size:
            rows = jnp.concatenate(
                [jnp.concatenate(left, axis=0), jnp.concatenate(right, axis=0)], axis=1
            )
            upper = jnp.concatenate(left, axis=0)
            turned = upper.T[rest:, :]
            work[rest:, :] = work[rest:, :] - dot(turned, rows, precision=HIGH)


def kernel(
    Z, X, Y,
    a_rank, b_rank, c_rank, al_hbm, ar_hbm, bl_hbm, br_hbm, pr_hbm,
    q_out, w_out,
    BL, BR, AL, AR, PR, ALT, PB, CO, CT, SM, SF, SG, ST, SU, ROWS, GS, GR, WK, NI, QB, PJ, LT, CF, CG, CT2, CU,
    in_sem, zs, zr, ps, pr, rs, rr, gs, gr, ns, nr, qs, qr,
):
    KD, COLS, NB, R = BL.shape
    PW = PR.shape[1]
    shard = bl_hbm.shape[2]
    part = NB // X
    halfpart = part // 2
    small_part = NB // (X * Y)
    pairs = COLS // 2
    r, q = lax.axis_index("row"), lax.axis_index("inner")
    z, c = r // 2, lax.rem(r, 2)
    x, y = q // Y, lax.rem(q, Y)
    up, down = lax.rem(z + 1, Z) * 2 + c, lax.rem(z + Z - 1, Z) * 2 + c
    mate = z * 2 + 1 - c
    peers = [(dx, 0) for dx in range(1, X)] + [(0, dy) for dy in range(1, Y)]

    def peer(dx, dy):
        return lax.rem(x + dx, X), lax.rem(y + dy, Y)

    barrier = pltpu.get_barrier_semaphore()
    ring_peers = [up, down] if Z > 2 else [up]
    for other in ring_peers + [mate]:
        pl.semaphore_signal(barrier, 1, device_id={"row": other, "inner": q}, device_id_type=MESH)
    for dx, dy in peers:
        px, py = peer(dx, dy)
        pl.semaphore_signal(barrier, 1, device_id={"row": r, "inner": px * Y + py}, device_id_type=MESH)

    mine = pl.ds(pl.multiple_of(r * shard, shard), shard)
    loads = [
        pltpu.make_async_copy(bl_hbm, BL.at[:, :, mine, :], in_sem.at[0]),
        pltpu.make_async_copy(br_hbm, BR.at[:, :, mine, :], in_sem.at[1]),
        pltpu.make_async_copy(ar_hbm.at[0], AR, in_sem.at[2]),
        pltpu.make_async_copy(al_hbm.at[0], AL, in_sem.at[3]),
        pltpu.make_async_copy(pr_hbm, PR, in_sem.at[4]),
    ]
    for load in loads:
        load.start()
    pl.semaphore_wait(barrier, len(ring_peers) + 1 + len(peers))

    tensors, given = (BL, BR), (bl_hbm, br_hbm)
    long_steps, short_steps = Z // 2, (Z - 1) // 2
    steps = ((long_steps, short_steps), (short_steps, long_steps))

    def rows_of(origin, core):
        return pl.ds(pl.multiple_of((origin * 2 + core) * shard, shard), shard)

    half = KD // CHUNKS

    def ring_copy(t, h, d, s, origin, own=False):
        ref = tensors[t].at[h * half : (h + 1) * half, :, rows_of(origin, c), :]
        src = given[t].at[h * half : (h + 1) * half] if own else ref
        return pltpu.make_async_remote_copy(
            src, ref, zs.at[t, h, d, s], zr.at[t, h, d, s],
            device_id={"row": down if d else up, "inner": q}, device_id_type=MESH,
        )

    def mate_copy(t, h, origin, core, own=False):
        ref = tensors[t].at[h * half : (h + 1) * half, :, rows_of(origin, core), :]
        src = given[t].at[h * half : (h + 1) * half] if own else ref
        return pltpu.make_async_remote_copy(
            src, ref, ps.at[t, h, origin], pr.at[t, h, origin],
            device_id={"row": mate, "inner": q}, device_id_type=MESH,
        )

    def sent_origin(d, s):
        return lax.rem(z + s, Z) if d else lax.rem(z + Z - s, Z)

    chunks = [(t, h) for t in range(2) for h in range(CHUNKS)]
    for t, h in chunks:
        for d in range(2):
            if steps[t][d]:
                ring_copy(t, h, d, 0, z, True).start()
    for t, h in chunks:
        mate_copy(t, h, z, c, True).start()

    loads[0].wait()
    loads[1].wait()
    loads[2].wait()
    loads[3].wait()
    loads[4].wait()
    CO[...] = jnp.zeros(CO.shape, F32)
    PB[...] = jnp.zeros(PB.shape, F32)

    def turn(k):
        at = pl.ds(pl.multiple_of(k * R, R), R)
        ALT[at, :] = AL[k].T

    def mate_wait(origins):
        for o in origins:
            for t, h in chunks:
                mate_copy(t, h, o, 1 - c).wait_recv()

    def absorb(origins):
        ats = [pl.ds(pl.multiple_of(o * 2 * shard, 2 * shard), 2 * shard) for o in origins]

        def stack(parts):
            return jnp.concatenate(parts, axis=0) if len(parts) > 1 else parts[0]

        probe = stack([PR[at, :] for at in ats]).T

        def body(k, carry):
            lhs = stack([AR[k, at, :] for at in ats]).T
            for g in range(pairs):
                for ref, left, total in ((BL, lhs, CO), (BR, probe, PB)):
                    rhs = jnp.concatenate(
                        [stack([ref[k, 2 * g + h, at, :] for at in ats]) for h in range(2)], axis=1
                    )
                    total[k, g] += dot(left, rhs)
            return carry

        lax.fori_loop(0, KD, body, 0)

    def hop(s, forward):
        for t, h in chunks:
            for d in range(2):
                if isinstance(s, int) and s >= steps[t][d]:
                    continue
                origin = sent_origin(d, s + 1)
                ring_copy(t, h, d, s, origin).wait_recv()
                if forward or (isinstance(s, int) and s + 1 < steps[t][d]):
                    ring_copy(t, h, d, s + 1, origin).start()
                mate_copy(t, h, origin, c).start()

    def both(s):
        return sent_origin(0, s), sent_origin(1, s)

    uniform = max(short_steps - 1, 0)
    if uniform:
        hop(0, True)
        mate_wait([z])
        absorb([z])

        def hop_loop(s, carry):
            hop(s, True)

            @pl.when(s < KD + 1)
            def _():
                turn(s - 1)

            mate_wait(both(s))
            absorb(both(s))
            return carry

        lax.fori_loop(1, uniform, hop_loop, 0)
        for k in range(min(uniform - 1, KD), KD):
            turn(k)
        done = uniform
    else:
        for k in range(KD):
            turn(k)
        mate_wait([z])
        absorb([z])
        done = 1
    for s in range(uniform, long_steps):
        hop(s, False)
        if 1 <= s:
            mate_wait(both(s))
            absorb(both(s))
    if Z > 1:
        last = [sent_origin(0, long_steps)]
        if short_steps == long_steps:
            last.append(sent_origin(1, long_steps))
        mate_wait(last)
        absorb(last)

    row_lane = lax.broadcasted_iota(jnp.int32, (R, R), 0)
    col_lane = lax.broadcasted_iota(jnp.int32, (R, R), 1)

    def cores(k, carry):
        at = pl.ds(pl.multiple_of(k * R, R), R)
        for j in range(COLS):
            g, at_j = j // 2, slice((j % 2) * R, (j % 2 + 1) * R)
            keep = jnp.logical_and(row_lane < a_rank[0, k], col_lane < b_rank[k, j])
            core = jnp.where(keep, CO[k, g, :, at_j], 0.0)
            CO[k, g, :, at_j] = core
            small = dot3(core, PB[k, g, :, at_j], ((1,), (1,)))
            SM[at, j * PW : (j + 1) * PW] = small.astype(BF16)
        return carry

    lax.fori_loop(0, KD, cores, 0)

    size, me = (X, Y), (x, y)

    def line(p, d):
        px, py = (lax.rem(x + d, X), y) if p == 0 else (x, lax.rem(y + d, Y))
        return {"row": r, "inner": px * Y + py}

    def first_copy(i, F, G, p, d):
        return pltpu.make_async_remote_copy(
            F.at[p, lax.rem(me[p] + d, size[p])], G.at[p, d], rs.at[i, 0, p, d], rr.at[i, 0, p, d],
            device_id=line(p, d), device_id_type=MESH,
        )

    def second_copy(i, T, U, p, d):
        return pltpu.make_async_remote_copy(
            T.at[p, lax.rem(me[1 - p] + d, size[1 - p])], U.at[p, d], rs.at[i, 1, p, d], rr.at[i, 1, p, d],
            device_id=line(1 - p, d), device_id_type=MESH,
        )

    def spread(i, compute, F, G):
        def body(d, carry):
            compute(lax.rem(x + d, X))
            first_copy(i, F, G, 0, d).start()
            return carry

        lax.fori_loop(1, X, body, 0)
        compute(x)
        for d in range(1, Y):
            first_copy(i, F, G, 1, d).start()

    def middle(i, F, G, T, U):
        for p in range(2):
            for d in range(1, size[p]):
                first_copy(i, F, G, p, d).wait_recv()

            def body(d, carry):
                o = lax.rem(me[1 - p] + d, size[1 - p])
                total = F[p, me[p], o].astype(F32)
                for e in range(1, size[p]):
                    total = total + G[p, e, o].astype(F32)
                T[p, o] = total.astype(BF16)
                return carry

            lax.fori_loop(1, size[1 - p] + 1, body, 0)
            for d in range(1, size[1 - p]):
                second_copy(i, T, U, p, d).start()

    def final(i, T, U, p):
        total = T[p, me[1 - p]].astype(F32)
        for d in range(1, size[1 - p]):
            second_copy(i, T, U, p, d).wait_recv()
            total = total + U[p, d].astype(F32)
        return total

    def sketch_rows(px):
        at = pl.ds(pl.multiple_of(px * part, part), part)
        lhs = jnp.concatenate([AL[k, at, :] for k in range(KD)], axis=1)
        rows = dot(lhs, SM[...]).astype(BF16)
        for j in range(COLS):
            SF[0, px, j] = rows[:halfpart, j * PW : (j + 1) * PW]
            SF[1, j, px] = rows[halfpart:, j * PW : (j + 1) * PW]

    spread(0, sketch_rows, SF, SG)

    for t, h in chunks:
        for d in range(2):
            for s in range(steps[t][d]):
                ring_copy(t, h, d, s, z).wait_send()

        def sent(o, carry):
            mate_copy(t, h, o, c).wait_send()
            return carry

        lax.fori_loop(0, Z, sent, 0)

    def turn_cores(k, carry):
        for j in range(COLS):
            CT[k, j] = CO[k, j // 2, :, (j % 2) * R : (j % 2 + 1) * R].T
        return carry

    lax.fori_loop(0, KD, turn_cores, 0)

    middle(0, SF, SG, ST, SU)
    for p in range(2):
        ROWS[p * halfpart : (p + 1) * halfpart, :] = final(0, ST, SU, p)

    own_rows = ROWS[...]
    GS[...] = dot(own_rows.T, own_rows, precision=HIGH)

    def gram_copy(dx):
        px = lax.rem(x + dx, X)
        return pltpu.make_async_remote_copy(
            GS, GR.at[dx], gs.at[dx], gr.at[dx],
            device_id={"row": r, "inner": px * Y + y}, device_id_type=MESH,
        )

    for dx in range(1, X):
        gram_copy(dx).start()

    for p in range(2):
        QB[y, x, p] = own_rows[p * halfpart : (p + 1) * halfpart, :].astype(BF16)

    def share_copy(step, p, d, sx, sy):
        if step == 0:
            ref = QB.at[sy, sx, p]
        else:
            ref = QB.at[sy, :, 0] if p == 0 else QB.at[:, sx, 1]
        return pltpu.make_async_remote_copy(
            ref, ref, qs.at[step, p, d], qr.at[step, p, d],
            device_id=line(p if step == 0 else 1 - p, d), device_id_type=MESH,
        )

    def share_wait(step, p):
        along = p if step == 0 else 1 - p
        for d in range(1, size[along]):
            sx = lax.rem(x + X - d, X) if along == 0 else x
            sy = lax.rem(y + Y - d, Y) if along == 1 else y
            share_copy(step, p, d, sx, sy).wait_recv()

    def share_start(step, p):
        for d in range(1, size[p if step == 0 else 1 - p]):
            share_copy(step, p, d, x, y).start()

    share_start(0, 0)
    share_start(0, 1)
    for p in range(2):
        share_wait(0, p)
        share_start(1, p)

    gram = GS[...]
    for dx in range(1, X):
        gram_copy(dx).wait_recv()
        gram = gram + GR[dx]
    eye = row_lane == col_lane
    mean = jnp.sum(jnp.where(eye, gram, 0.0), keepdims=True) / PW
    gram = gram + jnp.where(eye, 0.0001 * mean, 0.0)
    WK[:, 0:PW] = gram
    WK[:, PW : 2 * PW] = jnp.where(eye, 1.0, 0.0)
    factor(WK)
    NI[y] = WK[:, PW : 2 * PW]

    def inverse_copy(dy, sy, py):
        return pltpu.make_async_remote_copy(
            NI.at[sy], NI.at[sy], ns.at[dy], nr.at[dy],
            device_id={"row": r, "inner": x * Y + py}, device_id_type=MESH,
        )

    for dy in range(1, Y):
        inverse_copy(dy, y, lax.rem(y + dy, Y)).start()
    for p in range(2):
        share_wait(1, p)

    for g in range(pairs):
        PJ[:, 2 * g * PW : (2 * g + 2) * PW] = dot(
            ALT[...], jnp.concatenate([QB[2 * g + h].reshape(NB, PW) for h in range(2)], axis=1)
        )
    for dy in range(1, Y):
        inverse_copy(dy, lax.rem(y + Y - dy, Y), y).wait_recv()

    def orthonormal(rows, j):
        turned = dot3(rows, NI[j], ((1,), (1,)))
        lane = lax.broadcasted_iota(jnp.int32, turned.shape, 1)
        return jnp.where(lane < c_rank[0, j], turned, 0.0)

    for j in range(COLS):
        at_j = slice(j * PW, (j + 1) * PW)
        PJ[:, at_j] = orthonormal(PJ[:, at_j], j)

    def lift(k, carry):
        at = pl.ds(pl.multiple_of(k * R, R), R)
        for j in range(COLS):
            lifted = dot3(CT[k, j], PJ[at, j * PW : (j + 1) * PW])
            LT[at, j * PW : (j + 1) * PW] = lifted.astype(BF16)
        return carry

    lax.fori_loop(0, KD, lift, 0)

    def coeff_rows(px):
        at = pl.ds(pl.multiple_of(px * part, part), part)
        cut = small_part // 2
        for j in range(COLS):
            at_j = slice(j * PW, (j + 1) * PW)
            lhs = jnp.concatenate([BR[k, j, at, :] for k in range(KD)], axis=1)
            rows = dot(lhs, LT[:, at_j]).astype(BF16)
            for h in range(Y):
                CF[0, px, h, :, at_j] = rows[h * small_part : h * small_part + cut, :]
                CF[1, h, px, :, at_j] = rows[h * small_part + cut : (h + 1) * small_part, :]

    spread(1, coeff_rows, CF, CG)

    def exchange_sent(i, F, G, T, U):
        for p in range(2):
            for d in range(1, size[p]):
                first_copy(i, F, G, p, d).wait_send()
            for d in range(1, size[1 - p]):
                second_copy(i, T, U, p, d).wait_send()

    exchange_sent(0, SF, SG, ST, SU)
    for p in range(2):
        for step in range(2):
            for d in range(1, size[p if step == 0 else 1 - p]):
                share_copy(step, p, d, x, y).wait_send()
    for dx in range(1, X):
        gram_copy(dx).wait_send()
    for dy in range(1, Y):
        inverse_copy(dy, y, y).wait_send()
    for j in range(COLS):
        at_q = pl.ds(pl.multiple_of(lax.rem(y, Y // 2) * small_part, small_part), small_part)
        own = orthonormal(QB[j, x, y // (Y // 2), at_q, :].astype(F32), j)
        q_out[:, j * PW : (j + 1) * PW] = jnp.sqrt(jnp.float32(NB)) * own
    middle(1, CF, CG, CT2, CU)
    for p in range(2):
        cut = small_part // 2
        w_out[p * cut : (p + 1) * cut, :] = final(1, CT2, CU, p)

    exchange_sent(1, CF, CG, CT2, CU)


def per_device(Z, X, Y, a_left, a_right, a_rank, b_left, b_right, b_rank, c_rank, probes):
    _, KD, NB, R = a_left.shape
    COLS = b_left.shape[1]
    PW = probes.shape[1]
    part, small_part = NB // X, NB // (X * Y)
    m, half = max(X, Y), part // 2
    long_steps = max(Z // 2, 1)
    any_space = pl.BlockSpec(memory_space=pl.ANY)
    smem = pl.BlockSpec(memory_space=pltpu.SMEM)
    vmem = pl.BlockSpec(memory_space=pltpu.VMEM)
    dma = pltpu.SemaphoreType.DMA
    V = pltpu.VMEM
    out = jax.ShapeDtypeStruct((small_part, COLS * PW), F32)
    q_basis, w_factor = pl.pallas_call(
        functools.partial(kernel, Z, X, Y),
        out_shape=(out, out),
        in_specs=[smem] * 3 + [any_space] * 5,
        out_specs=(vmem, vmem),
        scratch_shapes=[
            V((KD, COLS, NB, R), BF16),
            V((KD, COLS, NB, R), BF16),
            V((KD, NB, R), BF16),
            V((KD, NB, R), BF16),
            V((NB, PW), BF16),
            V((KD * R, NB), BF16),
            V((KD, COLS // 2, PW, 2 * R), F32),
            V((KD, COLS // 2, R, 2 * R), F32),
            V((KD, COLS, R, R), F32),
            V((KD * R, COLS * PW), BF16),
            V((2, m, m, half, PW), BF16),
            V((2, m, m, half, PW), BF16),
            V((2, m, half, PW), BF16),
            V((2, m, half, PW), BF16),
            V((part, PW), F32),
            V((PW, PW), F32),
            V((X, PW, PW), F32),
            V((PW, 2 * PW), F32),
            V((COLS, PW, PW), F32),
            V((COLS, X, 2, half, PW), BF16),
            V((KD * R, COLS * PW), F32),
            V((KD * R, COLS * PW), BF16),
            V((2, m, m, small_part // 2, COLS * PW), BF16),
            V((2, m, m, small_part // 2, COLS * PW), BF16),
            V((2, m, small_part // 2, COLS * PW), BF16),
            V((2, m, small_part // 2, COLS * PW), BF16),
            dma((5,)),
            dma((2, CHUNKS, 2, long_steps)), dma((2, CHUNKS, 2, long_steps)),
            dma((2, CHUNKS, Z)), dma((2, CHUNKS, Z)),
            dma((2, 2, 2, m)), dma((2, 2, 2, m)),
            dma((X,)), dma((X,)),
            dma((Y,)), dma((Y,)),
            dma((2, 2, m)), dma((2, 2, m)),
        ],
        compiler_params=pltpu.CompilerParams(collective_id=0, has_side_effects=True),
    )(a_rank, b_rank, c_rank, a_left, a_right, b_left, b_right, probes)
    return q_basis.astype(BF16)[None], w_factor.astype(BF16)[None]


def solution(mesh):
    Z = mesh.shape["row"] // 2
    Y = 4
    X = mesh.shape["inner"] // Y
    return jax.shard_map(
        functools.partial(per_device, Z, X, Y),
        mesh=mesh,
        in_specs=(
            P("row", "inner", None, None),
            P("row", "inner", None, None),
            P("row", "inner"),
            P("inner", None, "row", None),
            P("inner", None, "row", None),
            P("inner", None),
            P("row", None),
            P(),
        ),
        out_specs=(P("row", "inner", None), P("row", "inner", None)),
        check_vma=False,
    )
```
